32 devices in a mesh: row: 8 (over z, x), col: 4 (over y, core).
Axes of the slice: x: 2, y: 2, z: 4, core: 2. Of those that a mesh axis runs over, the one named last changes fastest.
Arguments:
- snapshots: float32 [16384, 4096], P('row', 'col'), may hold values from -1.5 to 1.5
- tests: float32 [2, 4096, 128], P(None, 'col'), may hold values from -0.09375 to 0.09375
Outputs:
- basis: float32 [16384, 256], P('row')
- coeffs: float32 [256, 4096], P(None, 'col')
The draws below stay inside these ranges and needn't reach their ends.
All inputs are finite; a program needn't handle non-finite values.
Results may differ from the reference program's by a relative error of at most 0.0003.
Values sent between devices are 32-bit elements; how exact they have to be, the bound alone decides.
No kernel may reach another device: no remote copies, remote signals or barrier semaphores. Data moves between devices by JAX's collectives and lax.ppermute only.
A program may use at most 128 MiB of HBM per device.

```python
import math
import jax
import jax.numpy as jnp
from jax import lax

N = 4096
P_SIZE = 128
PANELS = 2
ROWS = 16384


def block_levels(stream_key, extent, pieces, low, top_value):
    factor_of = 1.0
    for dim, parts in pieces:
        steps = jax.random.uniform(jax.random.fold_in(jax.random.fold_in(stream_key, 6), dim), (parts,), jnp.float32, low / len(pieces), top_value / len(pieces))
        factor_of = factor_of * jnp.repeat(jnp.exp(steps), extent[dim] // parts).reshape((-1,) + (1,) * (len(extent) - 1 - dim))
    return factor_of


def gaussian(key, extent, spread, limit, pieces=(), held_as=jnp.bfloat16):
    array = jax.random.normal(key, extent, jnp.float32) * spread
    if len(pieces) > 0:
        array = block_levels(key, extent, pieces, -0.22, 0.18) * array
    return jnp.clip(array, min=-limit, max=limit).astype(held_as)


def setup_inputs(seed: int = 0) -> dict:
    key_list = jax.random.split(jax.random.key(seed), 3)
    snapshots = gaussian(key_list[0], (ROWS, N), 0.25, 1.5, ((0, 8), (1, 4)), jnp.float32)
    tests = gaussian(key_list[1], (PANELS, N, P_SIZE), N ** -0.5, 0.09375, ((1, 4),), jnp.float32)
    return dict(snapshots=snapshots, tests=tests)


def full_dot(left, right):
    return jnp.dot(left.astype(jnp.float32), right.astype(jnp.float32), precision=lax.Precision.HIGHEST, preferred_element_type=jnp.float32)

def left_dot(left, right):
    return lax.dot_general(left.astype(jnp.float32), right.astype(jnp.float32), (((0,), (0,)), ((), ())), precision=lax.Precision.HIGHEST, preferred_element_type=jnp.float32)

def reference(snapshots, tests):
    total = snapshots.shape[0]
    root = math.sqrt(total)
    bases = []
    coeff_list = []
    for panel in range(PANELS):
        sketch = full_dot(snapshots, tests[panel])
        if bases:
            earlier = jnp.concatenate(bases, axis=1)
            earlier_coeffs = jnp.concatenate(coeff_list, axis=0)
            small = full_dot(earlier_coeffs, tests[panel])
            sketch = sketch - full_dot(earlier, small) / root
        gram = left_dot(sketch, sketch) / total
        lower = jnp.linalg.cholesky(gram)
        inverse = jax.scipy.linalg.solve_triangular(lower, jnp.eye(gram.shape[0], dtype=jnp.float32), lower=True)
        new_basis = full_dot(sketch, inverse.T)
        bases.append(new_basis)
        coeff_list.append(left_dot(new_basis, snapshots) / root)
    return (jnp.concatenate(bases, axis=1), jnp.concatenate(coeff_list, axis=0))
```

```python
import math

import jax
import jax.numpy as jnp
from jax import lax
from jax.sharding import PartitionSpec as P

FULL = lax.Precision.HIGHEST
FAST = lax.Precision.HIGH


def mul(left, right, precision=FULL):
    return jnp.dot(left, right, precision=precision, preferred_element_type=jnp.float32)


def left_mul(left, right, precision=FULL):
    return lax.dot_general(
        left, right, (((0,), (0,)), ((), ())), precision=precision, preferred_element_type=jnp.float32
    )


def factors(size):
    found = []
    while size > 1:
        radix = 2 if not found or size % 4 else 4
        if size % radix:
            return None
        found.append(radix)
        size //= radix
    return found


def shift(x, axis, size, stride, radix, step):
    pairs = []
    for i in range(size):
        digit = (i // stride) % radix
        pairs.append((i, i + ((digit + step) % radix - digit) * stride))
    return lax.ppermute(x, axis, pairs)


def piece(x, index, count):
    rows = x.shape[0] // count
    return lax.dynamic_slice_in_dim(x, index * rows, rows, 0)


def scatter_sum(x, axis, size, stride, radix):
    digit = (lax.axis_index(axis) // stride) % radix
    total = piece(x, digit, radix)
    for step in range(1, radix):
        total = total + shift(piece(x, (digit + step) % radix, radix), axis, size, stride, radix, step)
    return total


def gather(x, axis, size, stride, radix):
    digit = (lax.axis_index(axis) // stride) % radix
    got = [x] + [shift(x, axis, size, stride, radix, step) for step in range(1, radix)]
    stacked = jnp.concatenate(got[:1] + got[:0:-1], axis=0)
    return jnp.roll(stacked, digit * x.shape[0], axis=0)


def all_sum(x, axis):
    size = lax.axis_size(axis)
    radices = factors(size)
    if radices is None or x.shape[0] % (8 * size):
        return lax.psum(x, axis)
    stride = 1
    for radix in radices:
        x = scatter_sum(x, axis, size, stride, radix)
        stride *= radix
    for radix in reversed(radices):
        stride //= radix
        x = gather(x, axis, size, stride, radix)
    return x


def all_sum_small(x, axis):
    size = lax.axis_size(axis)
    if size & (size - 1):
        return lax.psum(x, axis)
    step = 1
    while step < size:
        x = x + lax.ppermute(x, axis, [(i, i ^ step) for i in range(size)])
        step *= 2
    return x


def inverse_factor(gram):
    lower = jnp.linalg.cholesky(gram)
    return jax.scipy.linalg.solve_triangular(lower, jnp.eye(gram.shape[0], dtype=jnp.float32), lower=True)


def per_device(snapshots, tests):
    total = snapshots.shape[0] * lax.axis_size("row")
    root = math.sqrt(total)
    panels = tests.shape[0]
    sketches, rows, grams = [], [], {}
    for i in range(panels):
        sketch = all_sum(mul(snapshots, tests[i], FAST), "col")
        sketches.append(sketch)
        parts = [left_mul(sketch, other) for other in sketches]
        parts = all_sum_small(jnp.concatenate(parts, axis=1), "row") / total
        for j in range(i + 1):
            grams[i, j] = parts[:, j * sketch.shape[1] : (j + 1) * sketch.shape[1]]
        rows.append(all_sum(left_mul(sketch, snapshots, FAST), "row"))
    bases, coeffs, weights = [], [], []
    for i in range(panels):
        rest = grams[i, i]
        lowers = []
        for j in range(i):
            lower = sum(lax.dot_general(grams[i, k], weights[j][k], (((1,), (1,)), ((), ())),
                                        precision=FULL, preferred_element_type=jnp.float32)
                        for k in range(j + 1))
            lowers.append(lower)
            rest = rest - lax.dot_general(lower, lower, (((1,), (1,)), ((), ())),
                                          precision=FULL, preferred_element_type=jnp.float32)
        inverse = inverse_factor(rest)
        block_row = []
        for k in range(i):
            mixed = sum(mul(lowers[j], weights[j][k]) for j in range(k, i))
            block_row.append(-mul(inverse, mixed))
        block_row.append(inverse)
        weights.append(block_row)
        bases.append(sum(lax.dot_general(sketches[k], block_row[k], (((1,), (1,)), ((), ())),
                                         precision=FAST, preferred_element_type=jnp.float32)
                         for k in range(i + 1)))
        coeffs.append(sum(mul(block_row[k], rows[k]) for k in range(i + 1)) / root)
    return jnp.concatenate(bases, axis=1), jnp.concatenate(coeffs, axis=0)


def solution(mesh):
    in_specs = (P("row", "col"), P(None, "col", None))
    out_specs = (P("row", None), P(None, "col"))
    return jax.shard_map(per_device, mesh=mesh, in_specs=in_specs, out_specs=out_specs, check_vma=False)
```

```python
import functools
import math

import jax
import jax.numpy as jnp
from jax import lax
from jax.experimental import pallas as pl
from jax.experimental.pallas import tpu as pltpu
from jax.sharding import PartitionSpec as P

FULL = lax.Precision.HIGHEST
BOTH = ("row", "col")
NN, TN, NT = ((1,), (0,)), ((0,), (0,)), ((1,), (1,))


def mul(left, right, dims, precision=FULL):
    return lax.dot_general(left, right, (dims, ((), ())), precision=precision, preferred_element_type=jnp.float32)


def once(left, right, dims):
    return lax.dot_general(left, right, (dims, ((), ())), preferred_element_type=jnp.float32)


def split(x):
    high = x.astype(jnp.bfloat16)
    return high, (x - high.astype(jnp.float32)).astype(jnp.bfloat16)


def block_rows(rows):
    return next(b for b in (256, 128, 64, 32, 16, 8, rows) if rows % b == 0)


def sketch_kernel(half_ref, a_ref, w_ref, out_ref, pair):
    width = w_ref.shape[1]

    @pl.when(pl.program_id(0) == 0)
    def _():
        high, low = split(w_ref[...])
        pair[:, :width] = high
        pair[:, width:] = low

    high, low = split(a_ref[...])
    wide = once(high, pair[...], NN)
    out_ref[...] = wide[:, :width] + wide[:, width:] + once(low, pair[:, :width], NN)


def sketch_half(half, snapshots, tests, panel):
    rows, depth = snapshots.shape
    width = tests.shape[2]
    tile = block_rows(rows // 2)
    blocks = rows // 2 // tile
    return pl.pallas_call(
        sketch_kernel,
        grid_spec=pltpu.PrefetchScalarGridSpec(
            num_scalar_prefetch=1,
            grid=(blocks,),
            in_specs=[
                pl.BlockSpec((tile, depth), lambda i, h: (h[0] * blocks + i, 0)),
                pl.BlockSpec((None, depth, width), lambda i, h: (panel, 0, 0)),
            ],
            out_specs=pl.BlockSpec((tile, width), lambda i, h: (i, 0)),
            scratch_shapes=[pltpu.VMEM((depth, 2 * width), jnp.bfloat16)],
        ),
        out_shape=jax.ShapeDtypeStruct((rows // 2, width), jnp.float32),
        cost_estimate=pl.CostEstimate(
            flops=3 * rows * depth * width, bytes_accessed=2 * rows * depth, transcendentals=0
        ),
        name="sketch",
    )(half, snapshots, tests)


def product_kernel(count, more, half_ref, a_ref, *refs):
    y_refs, refs = refs[:count], refs[count:]
    if more:
        c_in, g_in, c_ref, g_ref, gram = refs
    else:
        c_ref, g_ref, gram = refs
    width = y_refs[0].shape[1]
    step = pl.program_id(0)

    @pl.when(step == 0)
    def _():
        c_ref[...] = c_in[...] if more else jnp.zeros_like(c_ref)
        gram[...] = jnp.zeros_like(gram)

    highs, lows = zip(*(split(ref[...]) for ref in y_refs))
    left = jnp.concatenate([highs[-1], lows[-1]], axis=1)
    high, low = split(a_ref[...])
    tall = once(left, high, TN)
    c_ref[...] += tall[:width] + tall[width:] + once(highs[-1], low, TN)
    for j in range(count):
        square = once(left, jnp.concatenate([highs[j], lows[j]], axis=1), TN)
        square = square[:width] + square[width:]
        gram[:, j * width : (j + 1) * width] += square[:, :width] + square[:, width:]

    @pl.when(step == pl.num_programs(0) - 1)
    def _():
        g_ref[...] = g_in[...] + gram[...] if more else gram[...]


def product_half(half, snapshots, sketches, before=()):
    rows, depth = snapshots.shape
    width = sketches[0].shape[1]
    tile = block_rows(rows // 2)
    blocks = rows // 2 // tile
    count = len(sketches)
    whole = lambda i, h: (0, 0)
    c_spec = pl.BlockSpec((width, depth), whole)
    g_spec = pl.BlockSpec((width, count * width), whole)
    return pl.pallas_call(
        functools.partial(product_kernel, count, bool(before)),
        grid_spec=pltpu.PrefetchScalarGridSpec(
            num_scalar_prefetch=1,
            grid=(blocks,),
            in_specs=[pl.BlockSpec((tile, depth), lambda i, h: (h[0] * blocks + i, 0))]
            + [pl.BlockSpec((tile, width), lambda i, h: (i, 0))] * count
            + [c_spec, g_spec][: len(before)],
            out_specs=[c_spec, g_spec],
            scratch_shapes=[pltpu.VMEM((width, count * width), jnp.float32)],
        ),
        out_shape=[
            jax.ShapeDtypeStruct((width, depth), jnp.float32),
            jax.ShapeDtypeStruct((width, count * width), jnp.float32),
        ],
        cost_estimate=pl.CostEstimate(
            flops=3 * rows * depth * width, bytes_accessed=2 * rows * depth, transcendentals=0
        ),
        name="product",
    )(half, snapshots, *sketches, *before)


def eliminate(gram, work, block):
    n = gram.shape[0]
    wide = 2 * n
    work[:, :n] = gram
    rows = lax.broadcasted_iota(jnp.int32, (n, n), 0)
    lanes = lax.broadcasted_iota(jnp.int32, (n, n), 1)
    work[:, n:] = jnp.where(rows == lanes, 1.0, 0.0)
    for start in range(0, n, block):
        stop = start + block
        tile = work[start:stop, :]
        entry = {}
        for a in range(block):
            for c in range(a + 1):
                entry[a, c] = jnp.broadcast_to(tile[a : a + 1, start + c : start + c + 1], (1, wide))
        new = []
        for c in range(block):
            scale = lax.rsqrt(entry[c, c])
            for a in range(c + 1, block):
                entry[a, c] = entry[a, c] * scale
            for a in range(c + 1, block):
                for e in range(c + 1, a + 1):
                    entry[a, e] = entry[a, e] - entry[a, c] * entry[e, c]
            line = work[start + c : start + c + 1, :]
            for e in range(c):
                line = line - entry[c, e] * new[e]
            new.append(line * scale)
        solved = jnp.concatenate(new, axis=0)
        work[start:stop, :] = solved
        if stop < n:
            work[stop:, :] -= mul(solved[:, stop:n], solved, TN)
    return work[:, n:]


def first_kernel(total, g_ref, w_ref, work):
    w_ref[...] = eliminate(g_ref[...] / total, work, 16)


def first_factor(grams, total):
    n = grams.shape[0]
    return pl.pallas_call(
        functools.partial(first_kernel, total),
        out_shape=jax.ShapeDtypeStruct((n, n), jnp.float32),
        scratch_shapes=[pltpu.VMEM((n, 2 * n), jnp.float32)],
        cost_estimate=pl.CostEstimate(flops=1 << 22, bytes_accessed=1 << 24, transcendentals=n),
        name="factor",
    )(grams)


def second_kernel(total, g_ref, first_ref, mixed_ref, side_ref, w_ref, work):
    n = g_ref.shape[0]
    first = first_ref[...]
    lower = mul(g_ref[:, :n] / total, first, NT)
    mixed = mul(lower, first, NN)
    mixed_ref[...] = mixed
    last = eliminate(g_ref[:, n:] / total - mul(lower, lower, NT), work, 16)
    w_ref[...] = last
    side_ref[...] = -mul(last, mixed, NN)


def second_factor(grams, first, total):
    n = grams.shape[0]
    square = jax.ShapeDtypeStruct((n, n), jnp.float32)
    return pl.pallas_call(
        functools.partial(second_kernel, total),
        out_shape=[square] * 3,
        scratch_shapes=[pltpu.VMEM((n, 2 * n), jnp.float32)],
        cost_estimate=pl.CostEstimate(flops=1 << 22, bytes_accessed=1 << 24, transcendentals=n),
        name="factor",
    )(grams, first)


def basis_kernel(count, blocks, half_ref, *refs):
    own, other, weights, out_ref = refs[:count], refs[count : 2 * count], refs[2 * count : 3 * count], refs[-1]
    here = pl.program_id(0) < blocks

    def run(parts):
        total = 0.0
        for y_ref, w_ref in zip(parts, weights):
            high, low = split(y_ref[...])
            w_high, w_low = split(w_ref[...])
            total = total + (once(high, w_high, NT) + (once(high, w_low, NT) + once(low, w_high, NT)))
        out_ref[...] = total

    @pl.when(here)
    def _():
        run(own)

    @pl.when(jnp.logical_not(here))
    def _():
        run(other)


def basis_columns(half, own, other, weights, panels, before=None):
    rows, width = own[0].shape
    tile = rows // 2 if rows % 16 == 0 else rows
    blocks = rows // tile
    count = len(own)
    panel = count - 1
    w_spec = pl.BlockSpec((width, width), lambda i, h: (0, 0))
    operands = [half, *own, *other, *weights]
    in_specs = [pl.BlockSpec((tile, width), lambda i, h: (jnp.minimum(i, blocks - 1), 0))] * count
    in_specs += [pl.BlockSpec((tile, width), lambda i, h: (jnp.maximum(i - blocks, 0), 0))] * count
    in_specs += [w_spec] * count
    aliases = {}
    if before is not None:
        aliases = {len(operands): 0}
        operands.append(before)
        in_specs.append(pl.BlockSpec(memory_space=pl.ANY))

    def place(i, h):
        side = jnp.where(i < blocks, h[0], 1 - h[0])
        return side * blocks + lax.rem(i, blocks), panel

    return pl.pallas_call(
        functools.partial(basis_kernel, count, blocks),
        grid_spec=pltpu.PrefetchScalarGridSpec(
            num_scalar_prefetch=1, grid=(2 * blocks,), in_specs=in_specs, out_specs=pl.BlockSpec((tile, width), place)
        ),
        out_shape=jax.ShapeDtypeStruct((2 * rows, panels * width), jnp.float32),
        input_output_aliases=aliases,
        cost_estimate=pl.CostEstimate(
            flops=12 * rows * width * width * count, bytes_accessed=8 * rows * width * (count + 1), transcendentals=0
        ),
        name="basis",
    )(*operands)


def coeff_kernel(root, last, bit_ref, w_ref, mine_ref, other_ref, *refs):
    rows = mine_ref.shape[0]
    whole = refs[-1]
    whole[pl.ds(pl.multiple_of(bit_ref[0] * rows, rows), rows), :] = mine_ref[...]
    whole[pl.ds(pl.multiple_of((1 - bit_ref[0]) * rows, rows), rows), :] = other_ref[...]
    value = whole[...] / root
    if last:
        refs[2][...] = mul(w_ref[...], value - refs[0][...], NN)
    else:
        refs[0][...] = mul(w_ref[...], value, NN)
        refs[1][...] = value


def coeff_rows(bit, weight, mine, other, root, panels, take=None, before=None):
    rows, depth = mine.shape
    width = weight.shape[0]
    full = lambda a: pl.BlockSpec(a.shape, lambda i, b: (0, 0))
    operands = [bit, weight, mine, other]
    aliases = {}
    out_shape = [jax.ShapeDtypeStruct((panels * width, depth), jnp.float32)]
    if take is None:
        out_specs = [pl.BlockSpec((width, depth), lambda i, b: (0, 0))] * 2
        out_shape.append(jax.ShapeDtypeStruct((width, depth), jnp.float32))
    else:
        out_specs = [pl.BlockSpec((width, depth), lambda i, b: (1, 0))]
        operands += [take, before]
        aliases = {5: 0}
    in_specs = [full(a) for a in operands[1:5]]
    if take is not None:
        in_specs.append(pl.BlockSpec(memory_space=pl.ANY))
    return pl.pallas_call(
        functools.partial(coeff_kernel, root, take is not None),
        grid_spec=pltpu.PrefetchScalarGridSpec(
            num_scalar_prefetch=1,
            grid=(1,),
            in_specs=in_specs,
            out_specs=out_specs,
            scratch_shapes=[pltpu.VMEM((width, depth), jnp.float32)],
        ),
        out_shape=out_shape,
        input_output_aliases=aliases,
        cost_estimate=pl.CostEstimate(
            flops=12 * width * width * depth, bytes_accessed=16 * width * depth, transcendentals=0
        ),
        name="coeffs",
    )(*operands)


def swaps(size):
    found, low, k = [(1, 1)], 1, size.bit_length() - 1
    while low + 1 < k:
        found += [(1 << low, 3 << low), (3 << low, 2 << low)]
        low += 2
    if low < k:
        found.append((1 << low, 1 << low))
    return found[:k]


def parity(value):
    for by in (16, 8, 4, 2, 1):
        value = value ^ (value >> by)
    return value & 1


class Swap:
    def __init__(self, step, rows, cols):
        table = swaps(rows)
        own = [table[(step + turn) % len(table)] for turn in (0, 1)]
        self.pairs = [(r * cols + c, (r ^ own[c % 2][0]) * cols + c) for r in range(rows) for c in range(cols)]
        row, odd = lax.axis_index("row"), lax.axis_index("col") % 2
        self.bit = parity(row & jnp.where(odd == 0, own[0][1], own[1][1]))

    def __call__(self, x):
        return lax.ppermute(x, BOTH, self.pairs)


def half(x, which):
    rows = x.shape[0] // 2
    return lax.dynamic_slice_in_dim(x, which * rows, rows, 0)


def join(mine, other, bit):
    return jnp.where(bit == 0, jnp.concatenate([mine, other]), jnp.concatenate([other, mine]))


def row_sum(x, small, rows, cols):
    cut = []
    for s in range(rows.bit_length() - 1):
        step = Swap(s, rows, cols)
        small_got = step(small)
        if x.shape[0] >= 16:
            cut.append(step)
            x = half(x, step.bit) + step(half(x, 1 - step.bit))
        else:
            x = x + step(x)
        small = small + small_got

    def finish():
        y = x
        for step in reversed(cut[1:]):
            y = join(y, step(y), step.bit)
        return cut[0].bit.reshape(1), y, cut[0](y)

    return small, finish


def per_device(snapshots, tests):
    rows, cols = lax.axis_size("row"), lax.axis_size("col")
    total = snapshots.shape[0] * rows
    root = math.sqrt(total)
    panels = tests.shape[0]
    core = (lax.axis_index("col") & 1).astype(jnp.int32).reshape(1)
    away = 1 - core

    def near(x):
        return lax.ppermute(x, "col", [(i, i ^ 1) for i in range(cols)])

    def far_sum(x):
        mask = 2
        while mask < cols:
            x = x + lax.ppermute(x, "col", [(i, i ^ mask) for i in range(cols)])
            mask *= 2
        return x

    def partial(panel):
        got = near(sketch_half(away, snapshots, tests, panel))
        return sketch_half(core, snapshots, tests, panel) + got

    part0, part1 = partial(0), partial(1)
    own0 = far_sum(part0)
    part1, own0 = lax.optimization_barrier((part1, own0))
    own1 = far_sum(part1)

    other0 = near(own0)
    rows0, gram0 = product_half(away, snapshots, [other0], product_half(core, snapshots, [own0]))
    gram0, finish0 = row_sum(rows0, gram0, rows, cols)
    weight0 = first_factor(gram0, total)

    other1 = near(own1)
    rows1, gram1 = product_half(
        away, snapshots, [other0, other1], product_half(core, snapshots, [own0, own1])
    )
    gram1, finish1 = row_sum(rows1, gram1, rows, cols)
    mixed, side, weight1 = second_factor(gram1, weight0, total)

    basis = basis_columns(core, [own0], [other0], [weight0], panels)
    coeffs, first_rows = coeff_rows(*[finish0()[0], weight0, *finish0()[1:]], root, panels)
    take = mul(mixed, first_rows, NN)
    basis = basis_columns(core, [own0, own1], [other0, other1], [side, weight1], panels, basis)
    bit, mine, other = finish1()
    coeffs = coeff_rows(bit, weight1, mine, other, root, panels, take, coeffs)[0]
    return basis, coeffs


def solution(mesh):
    in_specs = (P("row", "col"), P(None, "col", None))
    out_specs = (P("row", None), P(None, "col"))
    return jax.shard_map(per_device, mesh=mesh, in_specs=in_specs, out_specs=out_specs, check_vma=False)
```
